32 devices in a mesh: scene: 4 (over y, core), seg: 8 (over z, x).
Axes of the slice: x: 2, y: 2, z: 4, core: 2. Of those that a mesh axis runs over, the one named last changes fastest.
Arguments:
- points: bfloat16 [49152, 512], P(('scene', 'seg')), may hold values from -6 to 6
- zorder: int32 [384], P(('scene', 'seg')), may hold values from 0 to 383, as said below
- image: bfloat16 [4096, 1024], P(('scene', 'seg')), may hold values from -6 to 6
- image_row: int32 [49152], P(('scene', 'seg')), may hold values from 0 to 4095, as said below
- image_weight: bfloat16 [1024, 512], replicated, may hold values from -0.1875 to 0.1875
- norm_gain: float32 [2, 2, 512], replicated, may hold values from 0.1 to 1.9
- in_weight: bfloat16 [2, 512, 1536], replicated, may hold values from -16 to 16
- out_weight: bfloat16 [2, 512, 512], replicated, may hold values from -0.25 to 0.25
- up_weight: bfloat16 [2, 512, 2048], replicated, may hold values from -0.25 to 0.25
- down_weight: bfloat16 [2, 2048, 512], replicated, may hold values from -0.125 to 0.125
- hilbert_target: int32 [384], P(('scene', 'seg')), may hold values from 0 to 383, as said below
Outputs:
- features: bfloat16 [49152, 512], P(('scene', 'seg'))
The draws below stay inside these ranges and needn't reach their ends.
Inputs may be any that keep to these rules, and one draw needn't show every extreme that they name: zorder holds, for each device, a permutation of that device's 12 global block numbers. `image_row`: the row lies on a device of any scene group whose seg index equals that of the point's device. Within each scene group hilbert_target is a permutation of the group's block numbers; of one device's blocks at most 2 go to any one device, and in every draw some device hands exactly 2 blocks to another.
All inputs are finite; a program needn't handle non-finite values.
Results may differ from the reference program's by a relative error of at most 0.019.
Values may be sent and summed in bfloat16 or wider, within the bound.
No kernel may reach another device: no remote copies, remote signals or barrier semaphores. Data moves between devices by JAX's collectives and lax.ppermute only.
A program may use at most 192 MiB of HBM per device.

```python
import jax
import jax.numpy as jnp
from jax import lax

C = 512
HID = 2048
IMGC = 1024
HEAD_DIM = 16
PATCH = 512
BLK = 128
LAYERS = 2
BLK_DEV = 12
IMG_DEV = 128
HEADS = 32
POINTS = 49152
BLOCKS = 384
IMG_ROWS = 4096
N_SCENE = 4
N_SEG = 8
DEVICES = 32


def draw_zorder(key, part):
    keys = jax.random.split(jax.random.fold_in(key, 3), DEVICES)
    perms = jax.vmap(lambda single: jax.random.permutation(single, BLK_DEV))(keys)
    base = jnp.arange(DEVICES, dtype=jnp.int32)[:, None] * BLK_DEV
    return (perms.astype(jnp.int32) + base).reshape(-1)


def draw_image_row(key, part):
    first, second = jax.random.split(jax.random.fold_in(key, 11))
    device = jnp.arange(POINTS, dtype=jnp.int32) // (BLK_DEV * BLK)
    segment = device % N_SEG
    group = jax.random.randint(first, (POINTS,), 0, N_SCENE, dtype=jnp.int32)
    offset = jax.random.randint(second, (POINTS,), 0, IMG_DEV, dtype=jnp.int32)
    chosen = (group * N_SEG + segment) * IMG_DEV + offset
    return chosen.at[0].set(0).at[POINTS - 1].set(IMG_ROWS - 1)


def group_targets(key, group):
    keys = jax.random.split(key, 5)
    labels = jax.random.permutation(keys[0], N_SEG).astype(jnp.int32)
    lowest = (BLK_DEV + 1) // 2
    highest = min(BLK_DEV - 1, N_SEG) + 1
    single = jax.random.randint(keys[1], (), lowest, highest, dtype=jnp.int32)
    index = jnp.arange(BLK_DEV, dtype=jnp.int32)
    index = jnp.where(index < single, index, index - single)
    offsets = labels[index]
    shuffles = jax.vmap(lambda one: jax.random.permutation(one, BLK_DEV))(jax.random.split(keys[2], N_SEG))
    mapping = jax.random.permutation(keys[3], N_SEG).astype(jnp.int32)
    sources = jnp.arange(N_SEG, dtype=jnp.int32)[:, None]
    target_seg = mapping[(sources + offsets[shuffles]) % N_SEG].reshape(-1)
    tiebreak = jax.random.permutation(keys[4], N_SEG * BLK_DEV).astype(jnp.int32)
    order = jnp.argsort(target_seg * (N_SEG * BLK_DEV) + tiebreak)
    inverse = jnp.argsort(order).astype(jnp.int32)
    slot = inverse - target_seg * BLK_DEV
    return (group * N_SEG + target_seg) * BLK_DEV + slot


def draw_hilbert_target(key, part):
    keys = jax.random.split(jax.random.fold_in(key, 17), N_SCENE)
    groups = jnp.arange(N_SCENE, dtype=jnp.int32)
    return jax.vmap(group_targets)(keys, groups).reshape(-1).astype(jnp.int32)


def draw_in_weight(key, part):
    keys = jax.random.split(jax.random.fold_in(key, 7), 1)
    base = jax.random.normal(keys[0], (LAYERS, C, 3 * C), jnp.float32) * C ** (-0.5)
    return jnp.clip(base, -16.0, 16.0).astype(jnp.bfloat16)


def block_levels(stream_key, dims, pieces, low, high):
    level = 1.0
    for axis_at, shards_of in pieces:
        draws = jax.random.uniform(jax.random.fold_in(jax.random.fold_in(stream_key, 6), axis_at), (shards_of,), jnp.float32, low / len(pieces), high / len(pieces))
        level = level * jnp.repeat(jnp.exp(draws), dims[axis_at] // shards_of).reshape((-1,) + (1,) * (len(dims) - 1 - axis_at))
    return level


def bell_draw(key, extent, scale, bound, pieces=(), held_as=jnp.bfloat16):
    drawn = scale * jax.random.normal(key, extent, jnp.float32)
    if pieces:
        drawn = drawn * block_levels(key, extent, pieces, -0.22, 0.18)
    return jnp.clip(drawn, -bound, bound).astype(held_as)


def setup_inputs(seed: int = 0) -> dict:
    splits = jax.random.split(jax.random.key(seed), 12)
    points = bell_draw(splits[0], (POINTS, C), 1.0, 6.0, ((0, 32),))
    zorder = draw_zorder(jax.random.fold_in(splits[11], 71), 0)
    image = bell_draw(splits[2], (IMG_ROWS, IMGC), 1.0, 6.0, ((0, 32),))
    image_row = draw_image_row(jax.random.fold_in(splits[11], 71), 0)
    image_weight = bell_draw(splits[4], (IMGC, C), IMGC ** -0.5, 0.1875)
    norm_gain = jnp.clip(1.0 + 0.18 * jax.random.normal(splits[5], (LAYERS, 2, C), jnp.float32), 0.1, 1.9)
    in_weight = draw_in_weight(jax.random.fold_in(splits[11], 71), 0)
    out_weight = bell_draw(splits[7], (LAYERS, C, C), C ** -0.5, 0.25)
    up_weight = bell_draw(splits[8], (LAYERS, C, HID), C ** -0.5, 0.25)
    down_weight = bell_draw(splits[9], (LAYERS, HID, C), HID ** -0.5, 0.125)
    hilbert_target = draw_hilbert_target(jax.random.fold_in(splits[11], 71), 0)
    return {"points": points, "zorder": zorder, "image": image, "image_row": image_row, "image_weight": image_weight, "norm_gain": norm_gain, "in_weight": in_weight, "out_weight": out_weight, "up_weight": up_weight, "down_weight": down_weight, "hilbert_target": hilbert_target}


def normed(values, gain):
    center = values - lax.optimization_barrier(jnp.mean(values, axis=-1, keepdims=True))
    spread = lax.optimization_barrier(jnp.mean(center * center, axis=-1, keepdims=True))
    return (center * lax.rsqrt(spread + 1e-05) * gain).astype(jnp.bfloat16)

def attend(triple):
    query = triple[:, :C].reshape(PATCH, HEADS, HEAD_DIM).astype(jnp.float32)
    keys = triple[:, C:2 * C].reshape(PATCH, HEADS, HEAD_DIM).astype(jnp.float32)
    values = triple[:, 2 * C:].reshape(PATCH, HEADS, HEAD_DIM).astype(jnp.float32)
    scores = jnp.einsum('qhd,khd->hqk', query, keys) * HEAD_DIM ** (-0.5)
    scores = scores - lax.optimization_barrier(jnp.max(scores, axis=-1, keepdims=True))
    raised = jnp.exp(scores)
    weights = (raised / lax.optimization_barrier(jnp.sum(raised, axis=-1, keepdims=True))).astype(jnp.bfloat16)
    weights = lax.optimization_barrier(weights)
    mixed = jnp.einsum('hqk,khd->qhd', weights.astype(jnp.float32), values)
    return mixed.reshape(PATCH, C).astype(jnp.bfloat16)

def layer(features, gain, in_weight, out_weight, up_weight, down_weight):
    normal_one = normed(features, gain[0])
    triple = jnp.dot(normal_one, in_weight, preferred_element_type=jnp.float32).astype(jnp.bfloat16)
    mixed = attend(triple)
    after = features + jnp.dot(mixed, out_weight, preferred_element_type=jnp.float32)
    normal_two = normed(after, gain[1])
    hidden = jax.nn.gelu(jnp.dot(normal_two, up_weight, preferred_element_type=jnp.float32), approximate=False).astype(jnp.bfloat16)
    return after + jnp.dot(hidden, down_weight, preferred_element_type=jnp.float32)

def reference(points, zorder, image, image_row, image_weight, norm_gain, in_weight, out_weight, up_weight, down_weight, hilbert_target):
    image_proj = jnp.dot(image, image_weight, preferred_element_type=jnp.float32).astype(jnp.bfloat16)
    image_proj = lax.optimization_barrier(image_proj)
    joined = points.astype(jnp.float32) + jnp.take(image_proj, image_row, axis=0).astype(jnp.float32)
    zfeat = jnp.take(joined.reshape(BLOCKS, BLK, C), zorder, axis=0).reshape(-1, PATCH, C)

    def first_layer(patch):
        return layer(patch, norm_gain[0], in_weight[0], out_weight[0], up_weight[0], down_weight[0]).astype(jnp.bfloat16)

    def second_layer(patch):
        return layer(patch.astype(jnp.float32), norm_gain[1], in_weight[1], out_weight[1], up_weight[1], down_weight[1]).astype(jnp.bfloat16)
    first = lax.map(first_layer, zfeat)
    first = lax.optimization_barrier(first)
    hilbert = jnp.zeros((BLOCKS, BLK, C), jnp.bfloat16).at[hilbert_target].set(first.reshape(BLOCKS, BLK, C))
    second = lax.map(second_layer, hilbert.reshape(-1, PATCH, C))
    return second.reshape(POINTS, C)
```

```python
import functools

import jax
import jax.numpy as jnp
from jax import lax
from jax.experimental import pallas as pl
from jax.experimental.pallas import tpu as pltpu
from jax.sharding import PartitionSpec as P

HEAD_DIM = 16
PATCH = 512
CAP = 2
LANES = 128
GROUP = LANES // HEAD_DIM
QK_SCALE = HEAD_DIM ** (-0.5) * 1.4426950408889634
SAFE = 86.0
F32 = jnp.float32
BF16 = jnp.bfloat16


def dot(a, b):
    return jnp.dot(a, b, preferred_element_type=F32)


def dot_nt(a, b):
    return lax.dot_general(a, b, (((1,), (1,)), ((), ())), preferred_element_type=F32)


def dot_tn(a, b):
    return lax.dot_general(a, b, (((0,), (0,)), ((), ())), preferred_element_type=F32)


def normed(values, gain):
    center = values - jnp.mean(values, axis=-1, keepdims=True)
    spread = jnp.mean(center * center, axis=-1, keepdims=True)
    return (center * lax.rsqrt(spread + 1e-05) * gain).astype(BF16)


def head_mask(h):
    lane = lax.broadcasted_iota(jnp.int32, (1, LANES), 1) // HEAD_DIM
    return (lane == h).astype(F32).astype(BF16)


def project(x, gain, w_in, wqt, wvt, qt, keys, vt, safe, slot):
    width = x.shape[1]
    heads = width // HEAD_DIM
    n = normed(x, gain)
    q = (dot_nt(wqt[...], n) * QK_SCALE).astype(BF16)
    k = dot(n, w_in[:, width : 2 * width]).astype(BF16)
    v = dot_nt(wvt[...], n).astype(BF16)
    qt[...] = q
    keys[...] = k
    for h in range(heads):
        vt[h, :HEAD_DIM, :] = v[h * HEAD_DIM : (h + 1) * HEAD_DIM]
    row_head = lax.broadcasted_iota(jnp.int32, (heads, width), 0)
    col_head = lax.broadcasted_iota(jnp.int32, (heads, width), 1) // HEAD_DIM
    blocks = (row_head == col_head).astype(F32).astype(BF16)
    q2 = jnp.max(dot(blocks, q * q))
    k2 = jnp.max(dot_nt(blocks, k * k))
    safe[slot] = (q2 * k2 * 1.05 <= SAFE * SAFE).astype(jnp.int32)


def attend(qt, keys, vt, mixed_t, safe):
    groups = qt.shape[0] // LANES

    def finish(head, p):
        o = dot(vt[head], p)
        at = pl.ds(pl.multiple_of(head * HEAD_DIM, HEAD_DIM), HEAD_DIM)
        mixed_t[at, :] = (o[:HEAD_DIM] / o[HEAD_DIM : HEAD_DIM + 1]).astype(BF16)

    @pl.when(safe)
    def _():
        @pl.loop(0, groups)
        def _(g):
            at = pl.ds(pl.multiple_of(g * LANES, LANES), LANES)
            k = keys[:, at]
            q = qt[at, :]

            def raised(h):
                return jnp.exp2(dot(k * head_mask(h), q)).astype(BF16)

            p = raised(0)
            for h in range(GROUP):
                later = raised(h + 1) if h + 1 < GROUP else None
                finish(g * GROUP + h, p)
                p = later

    @pl.when(jnp.logical_not(safe))
    def _():
        @pl.loop(0, groups)
        def _(g):
            at = pl.ds(pl.multiple_of(g * LANES, LANES), LANES)

            @pl.loop(0, GROUP)
            def _(h):
                s = dot(keys[:, at] * head_mask(h), qt[at, :])
                s = s - jnp.max(s, axis=0, keepdims=True)
                finish(g * GROUP + h, jnp.exp2(s).astype(BF16))


def close(x, mixed, gain, w_out, w_up, w_down):
    after = x + dot(mixed, w_out[...])
    n = normed(after, gain)
    hidden = w_up.shape[1]
    step = PATCH
    total = after
    for c in range(0, hidden, step):
        u = dot(n, w_up[:, c : c + step])
        h = (0.5 * u * (1.0 + lax.erf(u * 0.7071067811865476))).astype(BF16)
        total = total + dot(h, w_down[c : c + step, :])
    return total


def prepare(w_in, wqt, wvt, vt, width):
    wqt[...] = w_in[:, :width].T
    wvt[...] = w_in[:, 2 * width :].T
    ones = jnp.ones((HEAD_DIM, vt.shape[2]), BF16)
    for h in range(vt.shape[0]):
        vt[h, HEAD_DIM:, :] = ones


def partner(i, k, n):
    return i ^ k if n & (n - 1) == 0 else (i + k) % n


def origin(i, k, n):
    return i ^ k if n & (n - 1) == 0 else (i + n - k) % n


def offset_to(i, d, n):
    if n & (n - 1) == 0:
        return lax.bitwise_xor(i, d)
    return lax.rem(d - i + n, n)


def layer_kernel(scenes, segs, blocks, per, first, *refs):
    refs = list(refs)
    zorder = refs.pop(0)
    targets = [refs.pop(0) for _ in range(1 if first else segs)]
    if first:
        pts = [refs.pop(0) for _ in range(per)]
        rows = [refs.pop(0) for _ in range(per)]
        tables = [refs.pop(0) for _ in range(scenes)]
    else:
        arrived = [refs.pop(0) for _ in range(segs)]
    gains, w_in, w_out, w_up, w_down = [refs.pop(0) for _ in range(5)]
    outs = [refs.pop(0) for _ in range(segs if first else 1)]
    x, wqt, wvt, qt, keys, vt, mixed_t, flag, stage, sems = refs
    width = w_out.shape[0]
    p = pl.program_id(0)
    block = PATCH // per
    device = zorder[0] // blocks
    seg = lax.rem(device, segs)
    scene = device // segs

    if not first:

        @pl.when(p == 0)
        def _():
            for k in range(segs):
                seen = jnp.int32(0)
                for i in range(blocks):
                    t = targets[k][i]
                    mine = t // blocks == device
                    slot = lax.rem(t, blocks)
                    rank = seen

                    @pl.when(mine)
                    def _():
                        pltpu.make_async_copy(
                            arrived[k].at[rank], stage.at[slot], sems.at[slot]
                        ).start()

                    seen = seen + mine.astype(jnp.int32)

    @pl.when(p == 0)
    def _():
        prepare(w_in, wqt, wvt, vt, width)

    if first:
        for j in range(per):
            total = pts[j][...].astype(F32)
            index = rows[j][0]
            count = tables[0].shape[0]
            for k in range(scenes):
                group = origin_traced(scene, k, scenes)
                base = (group * segs + seg) * count
                entry = lax.broadcasted_iota(jnp.int32, (count, block), 0) + base
                pick = (entry == index).astype(F32).astype(BF16)
                total = total + dot_tn(pick, tables[k][...])
            x[j * block : (j + 1) * block, :] = total
    else:
        for j in range(per):
            at = p * per + j
            pltpu.make_async_copy(arrived[0].at[0], stage.at[at], sems.at[at]).wait()
            x[j * block : (j + 1) * block, :] = stage[at].astype(F32)

    project(x[...], gains[0:1], w_in, wqt, wvt, qt, keys, vt, flag, 0)
    attend(qt, keys, vt, mixed_t, flag[0] == 1)
    done = close(x[...], mixed_t[...].T, gains[1:2], w_out, w_up, w_down).astype(BF16)
    if not first:
        outs[0][...] = done
        return
    for j in range(per):
        stage[p * per + j] = done[j * block : (j + 1) * block]
    target = targets[0]
    for j in range(per):
        i = p * per + j
        mine = target[i] // blocks
        rank = jnp.int32(0)
        for e in range(blocks):
            same = jnp.logical_and(target[e] // blocks == mine, e < i)
            rank = rank + same.astype(jnp.int32)
        k = offset_to(seg, lax.rem(mine, segs), segs)
        for o in range(segs):

            @pl.when(k == o)
            def _():
                pltpu.make_async_copy(stage.at[i], outs[o].at[rank], sems.at[i]).start()

    @pl.when(p == pl.num_programs(0) - 1)
    def _():
        for i in range(blocks):
            pltpu.make_async_copy(stage.at[i], outs[0].at[0], sems.at[i]).wait()


def origin_traced(i, k, n):
    if n & (n - 1) == 0:
        return lax.bitwise_xor(i, jnp.int32(k))
    return lax.rem(i + (n - k), n)


def scratch(width, blocks, block):
    heads = width // HEAD_DIM
    return [
        pltpu.VMEM((PATCH, width), F32),
        pltpu.VMEM((width, width), BF16),
        pltpu.VMEM((width, width), BF16),
        pltpu.VMEM((width, PATCH), BF16),
        pltpu.VMEM((PATCH, width), BF16),
        pltpu.VMEM((heads, 2 * HEAD_DIM, PATCH), BF16),
        pltpu.VMEM((width, PATCH), BF16),
        pltpu.SMEM((1,), jnp.int32),
        pltpu.VMEM((blocks, block, width), BF16),
        pltpu.SemaphoreType.DMA((blocks,)),
    ]


def whole(shape):
    return pl.BlockSpec(shape, lambda *_: (0,) * len(shape), pipeline_mode=pl.Buffered(1))


def weight_specs(weights, layer):
    def spec(shape):
        return pl.BlockSpec((None,) + shape[1:], lambda *_: (layer,) + (0,) * (len(shape) - 1), pipeline_mode=pl.Buffered(1))

    return [spec(w.shape) for w in weights]


ANY = pl.BlockSpec(memory_space=pl.ANY)


def first_layer(scenes, segs, zorder, target, points, rows, tables, weights, layer=0):
    blocks = zorder.shape[0]
    length, width = points.shape
    block = length // blocks
    per = PATCH // block

    def at_block(j, rank):
        def index(p, z, t):
            return (lax.rem(z[p * per + j], blocks),) + (0,) * (rank - 1)

        return index

    return pl.pallas_call(
        functools.partial(layer_kernel, scenes, segs, blocks, per, True),
        grid_spec=pltpu.PrefetchScalarGridSpec(
            num_scalar_prefetch=2,
            grid=(length // PATCH,),
            in_specs=[pl.BlockSpec((block, width), at_block(j, 2)) for j in range(per)]
            + [pl.BlockSpec((1, 1, block), at_block(j, 3)) for j in range(per)]
            + [whole(t.shape) for t in tables]
            + weight_specs(weights, layer),
            out_specs=[ANY] * segs,
            scratch_shapes=scratch(width, blocks, block),
        ),
        out_shape=[jax.ShapeDtypeStruct((CAP, block, width), BF16)] * segs,
        compiler_params=pltpu.CompilerParams(vmem_limit_bytes=56 << 20),
    )(zorder, target, *[points] * per, *[rows.reshape(blocks, 1, block)] * per, *tables, *weights)


def second_layer(segs, zorder, targets, arrived, weights, layer=1):
    blocks = zorder.shape[0]
    _, block, width = arrived[0].shape
    per = PATCH // block
    length = blocks * block
    return pl.pallas_call(
        functools.partial(layer_kernel, 0, segs, blocks, per, False),
        grid_spec=pltpu.PrefetchScalarGridSpec(
            num_scalar_prefetch=1 + segs,
            grid=(length // PATCH,),
            in_specs=[ANY] * segs + weight_specs(weights, layer),
            out_specs=pl.BlockSpec((PATCH, width), lambda p, *_: (p, 0)),
            scratch_shapes=scratch(width, blocks, block),
        ),
        out_shape=jax.ShapeDtypeStruct((length, width), BF16),
        compiler_params=pltpu.CompilerParams(vmem_limit_bytes=56 << 20),
    )(zorder, *targets, *arrived, *weights)


def exchange(values, axis):
    n = lax.axis_size(axis)
    return [values[0]] + [
        lax.ppermute(values[k], axis, [(i, partner(i, k, n)) for i in range(n)])
        for k in range(1, n)
    ]


def local(points, zorder, image, image_row, image_weight, norm_gain, in_weight, out_weight, up_weight, down_weight, hilbert_target):
    scenes = lax.axis_size("scene")
    segs = lax.axis_size("seg")
    weights = (norm_gain, in_weight, out_weight, up_weight, down_weight)
    targets = exchange([hilbert_target] * segs, "seg")
    proj = dot(image, image_weight).astype(BF16)
    tables = exchange([proj] * scenes, "scene")
    sent = first_layer(scenes, segs, zorder, hilbert_target, points, image_row, tables, weights)
    arrived = exchange(sent, "seg")
    return second_layer(segs, zorder, targets, arrived, weights)


def solution(mesh):
    placed = (
        P(("scene", "seg"), None),
        P(("scene", "seg")),
        P(("scene", "seg"), None),
        P(("scene", "seg")),
        P(),
        P(),
        P(),
        P(),
        P(),
        P(),
        P(("scene", "seg")),
    )
    return jax.shard_map(local, mesh=mesh, in_specs=placed, out_specs=P(("scene", "seg"), None), check_vma=False)
```

```python
import functools

import jax
import jax.numpy as jnp
from jax import lax
from jax.experimental import pallas as pl
from jax.experimental.pallas import tpu as pltpu
from jax.sharding import PartitionSpec as P

HEAD_DIM = 16
PATCH = 512
CAP = 2
LANES = 128
GROUP = LANES // HEAD_DIM
QK_SCALE = HEAD_DIM ** (-0.5) * 1.4426950408889634
SAFE = 86.0
F32 = jnp.float32
BF16 = jnp.bfloat16


def dot(a, b):
    return jnp.dot(a, b, preferred_element_type=F32)


def dot_nt(a, b):
    return lax.dot_general(a, b, (((1,), (1,)), ((), ())), preferred_element_type=F32)


def dot_tn(a, b):
    return lax.dot_general(a, b, (((0,), (0,)), ((), ())), preferred_element_type=F32)


def normed(values, gain):
    center = values - jnp.mean(values, axis=-1, keepdims=True)
    spread = jnp.mean(center * center, axis=-1, keepdims=True)
    return (center * lax.rsqrt(spread + 1e-05) * gain).astype(BF16)


def head_mask(h):
    lane = lax.broadcasted_iota(jnp.int32, (1, LANES), 1) // HEAD_DIM
    return (lane == h).astype(F32).astype(BF16)


def project(x, gain, w_in, wqt, wvt):
    width = x.shape[1]
    heads = width // HEAD_DIM
    n = normed(x, gain)
    q = (dot_nt(wqt[...], n) * QK_SCALE).astype(BF16)
    k = dot(n, w_in[:, width : 2 * width]).astype(BF16)
    v = dot_nt(wvt[...], n).astype(BF16)
    row_head = lax.broadcasted_iota(jnp.int32, (heads, width), 0)
    col_head = lax.broadcasted_iota(jnp.int32, (heads, width), 1) // HEAD_DIM
    blocks = (row_head == col_head).astype(F32).astype(BF16)
    q2 = jnp.max(dot(blocks, q * q))
    k2 = jnp.max(dot_nt(blocks, k * k))
    return q, k, v, (q2 * k2 * 1.05 <= SAFE * SAFE).astype(jnp.int32)


def slab(i, size):
    return pl.ds(i * size if isinstance(i, int) else pl.multiple_of(i * size, size), size)


def weigh(vt, head, count, p):
    ones = jnp.ones((HEAD_DIM, vt.shape[1]), BF16)
    return dot(jnp.concatenate([vt[pl.ds(pl.multiple_of(head * HEAD_DIM, HEAD_DIM), count * HEAD_DIM), :], ones]), p)


def attend_patch(qt, keys, vt, mixed_t, safe):
    groups = qt.shape[0] // LANES

    def finish(head, p):
        o = weigh(vt, head, 1, p)
        mixed_t[slab(head, HEAD_DIM), :] = (o[:HEAD_DIM] / o[HEAD_DIM : HEAD_DIM + 1]).astype(BF16)

    @pl.when(safe)
    def _():
        @pl.loop(0, groups)
        def _(g):
            k = keys[:, slab(g, LANES)]
            q = qt[slab(g, LANES), :]

            def raised(h):
                return jnp.exp2(dot(k * head_mask(h), q)).astype(BF16)

            p = raised(0)
            for h in range(GROUP):
                later = raised(h + 1) if h + 1 < GROUP else None
                finish(g * GROUP + h, p)
                p = later

    @pl.when(jnp.logical_not(safe))
    def _():
        @pl.loop(0, groups)
        def _(g):
            @pl.loop(0, GROUP)
            def _(h):
                s = dot(keys[:, slab(g, LANES)] * head_mask(h), qt[slab(g, LANES), :])
                s = s - jnp.max(s, axis=0, keepdims=True)
                finish(g * GROUP + h, jnp.exp2(s).astype(BF16))


def attend_block(qt, keys, vt, mixed_t, safe):
    groups = qt.shape[0] // LANES
    side = 4
    rows = qt.shape[1]
    row_head = lax.broadcasted_iota(jnp.int32, (LANES, 1), 0) // HEAD_DIM

    def only(q, h):
        return q * (row_head == h).astype(F32).astype(BF16)

    @pl.when(safe)
    def _():
        def raised(step):
            g, part = divmod(step, GROUP // side)
            q = qt[slab(g, LANES), :]
            wide = jnp.concatenate([only(q, part * side + i) for i in range(side)], axis=1)
            return jnp.exp2(dot(keys[:, slab(g, LANES)], wide)).astype(BF16)

        def finish(step, p):
            for i in range(0, side, 2):
                head = step * side + i
                o = weigh(vt, head, 2, p[:, i * rows : (i + 2) * rows])
                for e in range(2):
                    part = slice(e * rows, (e + 1) * rows)
                    scaled = o[e * HEAD_DIM : (e + 1) * HEAD_DIM, part] / o[2 * HEAD_DIM : 2 * HEAD_DIM + 1, part]
                    mixed_t[slab(head + e, HEAD_DIM), :] = scaled.astype(BF16)

        steps = groups * GROUP // side
        p = raised(0)
        for step in range(steps):
            later = raised(step + 1) if step + 1 < steps else None
            finish(step, p)
            p = later

    @pl.when(jnp.logical_not(safe))
    def _():
        @pl.loop(0, groups)
        def _(g):
            @pl.loop(0, GROUP)
            def _(h):
                s = dot(keys[:, slab(g, LANES)], only(qt[slab(g, LANES), :], h))
                s = s - jnp.max(s, axis=0, keepdims=True)
                o = weigh(vt, g * GROUP + h, 1, jnp.exp2(s).astype(BF16))
                mixed_t[slab(g * GROUP + h, HEAD_DIM), :] = (o[:HEAD_DIM] / o[HEAD_DIM : HEAD_DIM + 1]).astype(BF16)


def close(x, mixed, gain, w_out, w_up, w_down):
    after = x + dot(mixed, w_out[...])
    n = normed(after, gain)
    hidden = w_up.shape[1]
    step = PATCH
    total = after
    for c in range(0, hidden, step):
        u = dot(n, w_up[:, c : c + step])
        h = (0.5 * u * (1.0 + lax.erf(u * 0.7071067811865476))).astype(BF16)
        total = total + dot(h, w_down[c : c + step, :])
    return total


def prepare(w_in, wqt, wvt):
    width = wqt.shape[0]
    wqt[...] = w_in[:, :width].T
    wvt[...] = w_in[:, 2 * width :].T


def partner(i, k, n):
    return i ^ k if n & (n - 1) == 0 else (i + k) % n


def origin(i, k, n):
    return i ^ k if n & (n - 1) == 0 else (i + n - k) % n


def offset_to(i, d, n):
    if n & (n - 1) == 0:
        return lax.bitwise_xor(i, d)
    return lax.rem(d - i + n, n)


def origin_traced(i, k, n):
    if n & (n - 1) == 0:
        return lax.bitwise_xor(i, jnp.int32(k))
    return lax.rem(i + (n - k), n)


def join_kernel(scenes, segs, blocks, per, *refs):
    refs = list(refs)
    zorder = refs.pop(0)
    pts = [refs.pop(0) for _ in range(per)]
    rows = [refs.pop(0) for _ in range(per)]
    tables = [refs.pop(0) for _ in range(scenes)]
    gains, w_in, x, qt, keys, vt, safe, wqt, wvt = refs
    block = x.shape[0] // per
    device = zorder[0] // blocks
    seg = lax.rem(device, segs)
    scene = device // segs
    p = pl.program_id(0)

    @pl.when(p == 0)
    def _():
        prepare(w_in, wqt, wvt)

    for j in range(per):
        total = pts[j][...].astype(F32)
        index = rows[j][0]
        count = tables[0].shape[0]
        for k in range(scenes):
            base = (origin_traced(scene, k, scenes) * segs + seg) * count
            entry = lax.broadcasted_iota(jnp.int32, (count, block), 0) + base
            pick = (entry == index).astype(F32).astype(BF16)
            total = total + dot_tn(pick, tables[k][...])
        x[j * block : (j + 1) * block, :] = total
    q, k, v, ok = project(x[...], gains[0:1], w_in, wqt, wvt)
    for j in range(per):
        qt[j] = q[:, j * block : (j + 1) * block]
    keys[...] = k
    vt[...] = v
    safe[p] = ok


def blocks_kernel(layer, segs, blocks, per, start, count, given, *refs):
    refs = list(refs)
    zorder, target, safe, x, qt, keys, vt, gains, w_out, w_up, w_down = [refs.pop(0) for _ in range(11)]
    left = len(refs) - 20 - given
    refs = refs[given:]
    outs = [refs.pop(0) for _ in range(left)]
    order, offset, rank, xs, qb, kb, vb, mt, mixed, stage, wo, wu, wd, qs, ks, vs, xsem, ws, os, _ = refs
    block = qt.shape[2]
    device = zorder[0] // blocks
    seg = lax.rem(device, segs)

    for i in range(blocks):
        offset[i] = offset_to(seg, lax.rem(target[i] // blocks, segs), segs)
    for i in range(blocks):
        mine = offset[i]
        place = jnp.int32(0)
        same = jnp.int32(0)
        for e in range(blocks):
            if e != i:
                place = place + (offset[e] > mine).astype(jnp.int32)
            if e < i:
                same = same + (offset[e] == mine).astype(jnp.int32)
        rank[i] = same
        order[place + same] = jnp.int32(i)

    def fetch(j, slot):
        i = order[start + j]
        return (
            pltpu.make_async_copy(qt.at[i], qb.at[slot], qs.at[slot]),
            pltpu.make_async_copy(keys.at[i // per], kb.at[slot], ks.at[slot]),
            pltpu.make_async_copy(vt.at[i // per], vb.at[slot], vs.at[slot]),
        )

    for copy in fetch(0, 0):
        copy.start()
    late = [
        pltpu.make_async_copy(w.at[layer], held, ws.at[n])
        for n, (w, held) in enumerate(((w_out, wo), (w_up, wu), (w_down, wd)))
    ]
    for j in range(count):
        late.append(pltpu.make_async_copy(x.at[slab(order[start + j], block), :], xs.at[slab(j, block), :], xsem.at[j]))
    for copy in late:
        copy.start()

    @pl.loop(0, count)
    def _(j):
        slot = lax.rem(j, 2)

        @pl.when(j + 1 < count)
        def _():
            for copy in fetch(j + 1, 1 - slot):
                copy.start()

        for copy in fetch(j, slot):
            copy.wait()
        attend_block(qb.at[slot], kb.at[slot], vb.at[slot], mt, safe[order[start + j] // per] == 1)
        mixed[slab(j, block), :] = mt[...].T

    for copy in late:
        copy.wait()
    done = close(xs[...], mixed[...], gains[1:2], wo, wu, wd).astype(BF16)
    for j in range(count):
        stage[j] = done[j * block : (j + 1) * block]
        i = order[start + j]
        for n in range(left):
            o = left - 1 - n

            @pl.when(offset[i] == o)
            def _():
                pltpu.make_async_copy(stage.at[j], outs[n].at[rank[i]], os.at[j]).start()

    for j in range(count):
        pltpu.make_async_copy(stage.at[j], outs[0].at[0], os.at[j]).wait()


def patch_kernel(segs, blocks, per, *refs):
    refs = list(refs)
    zorder = refs.pop(0)
    targets = [refs.pop(0) for _ in range(segs)]
    arrived = [refs.pop(0) for _ in range(segs)]
    gains, w_in, w_out, w_up, w_down, out, x, wqt, wvt, qt, keys, vt, mixed_t, stage, sems = refs
    p = pl.program_id(0)
    block = PATCH // per
    device = zorder[0] // blocks

    @pl.when(p == 0)
    def _():
        for k in range(segs):
            seen = jnp.int32(0)
            for i in range(blocks):
                t = targets[k][i]
                mine = t // blocks == device
                slot = lax.rem(t, blocks)
                rank = seen

                @pl.when(mine)
                def _():
                    pltpu.make_async_copy(arrived[k].at[rank], stage.at[slot], sems.at[slot]).start()

                seen = seen + mine.astype(jnp.int32)
        prepare(w_in, wqt, wvt)

    for j in range(per):
        at = p * per + j
        pltpu.make_async_copy(arrived[0].at[0], stage.at[at], sems.at[at]).wait()
        x[j * block : (j + 1) * block, :] = stage[at].astype(F32)
    qt[...], keys[...], vt[...], ok = project(x[...], gains[0:1], w_in, wqt, wvt)
    attend_patch(qt, keys, vt, mixed_t, ok == 1)
    out[...] = close(x[...], mixed_t[...].T, gains[1:2], w_out, w_up, w_down).astype(BF16)


def whole(shape):
    return pl.BlockSpec(shape, lambda *_: (0,) * len(shape), pipeline_mode=pl.Buffered(1))


def of_layer(layer, array):
    shape = array.shape
    return pl.BlockSpec((None,) + shape[1:], lambda *_: (layer,) + (0,) * (len(shape) - 1), pipeline_mode=pl.Buffered(1))


ANY = pl.BlockSpec(memory_space=pl.ANY)
SEMS = pltpu.SemaphoreType.DMA


def joined(scenes, segs, zorder, points, rows, tables, gains, w_in):
    blocks = zorder.shape[0]
    length, width = points.shape
    block = length // blocks
    per = PATCH // block
    patches = length // PATCH

    def at_block(j, rank):
        def index(p, z):
            return (lax.rem(z[p * per + j], blocks),) + (0,) * (rank - 1)

        return index

    return pl.pallas_call(
        functools.partial(join_kernel, scenes, segs, blocks, per),
        grid_spec=pltpu.PrefetchScalarGridSpec(
            num_scalar_prefetch=1,
            grid=(patches,),
            in_specs=[pl.BlockSpec((block, width), at_block(j, 2)) for j in range(per)]
            + [pl.BlockSpec((1, 1, block), at_block(j, 3)) for j in range(per)]
            + [whole(t.shape) for t in tables]
            + [of_layer(0, gains), of_layer(0, w_in)],
            out_specs=[
                pl.BlockSpec((PATCH, width), lambda p, *_: (p, 0)),
                pl.BlockSpec((per, width, block), lambda p, *_: (p, 0, 0)),
                pl.BlockSpec((None, PATCH, width), lambda p, *_: (p, 0, 0)),
                pl.BlockSpec((None, width, PATCH), lambda p, *_: (p, 0, 0)),
                pl.BlockSpec(memory_space=pltpu.SMEM),
            ],
            scratch_shapes=[pltpu.VMEM((width, width), BF16)] * 2,
        ),
        out_shape=[
            jax.ShapeDtypeStruct((length, width), F32),
            jax.ShapeDtypeStruct((blocks, width, block), BF16),
            jax.ShapeDtypeStruct((patches, PATCH, width), BF16),
            jax.ShapeDtypeStruct((patches, width, PATCH), BF16),
            jax.ShapeDtypeStruct((patches,), jnp.int32),
        ],
        compiler_params=pltpu.CompilerParams(vmem_limit_bytes=40 << 20),
    )(zorder, *[points] * per, *[rows.reshape(blocks, 1, block)] * per, *tables, gains, w_in)


def some_blocks(start, count, segs, left, zorder, target, state, gains, weights, sofar):
    x, qt, keys, vt, safe = state
    blocks = zorder.shape[0]
    _, width, block = qt.shape
    per = PATCH // block
    hidden = weights[1].shape[2]
    given = len(sofar)
    first = 11
    return pl.pallas_call(
        functools.partial(blocks_kernel, 0, segs, blocks, per, start, count, given),
        grid_spec=pltpu.PrefetchScalarGridSpec(
            num_scalar_prefetch=3,
            grid=(1,),
            in_specs=[ANY] * 4 + [of_layer(0, gains)] + [ANY] * (3 + given),
            out_specs=[ANY] * left,
            scratch_shapes=[pltpu.SMEM((blocks,), jnp.int32)] * 3
            + [
                pltpu.VMEM((count * block, width), F32),
                pltpu.VMEM((2, width, block), BF16),
                pltpu.VMEM((2, PATCH, width), BF16),
                pltpu.VMEM((2, width, PATCH), BF16),
                pltpu.VMEM((width, block), BF16),
                pltpu.VMEM((count * block, width), BF16),
                pltpu.VMEM((count, block, width), BF16),
                pltpu.VMEM((width, width), BF16),
                pltpu.VMEM((width, hidden), BF16),
                pltpu.VMEM((hidden, width), BF16),
                SEMS((2,)),
                SEMS((2,)),
                SEMS((2,)),
                SEMS((count,)),
                SEMS((3,)),
                SEMS((count,)),
                SEMS((1,)),
            ],
        ),
        out_shape=[jax.ShapeDtypeStruct((CAP, block, width), BF16)] * left,
        input_output_aliases={first + given - left + n: n for n in range(left)} if given else {},
        compiler_params=pltpu.CompilerParams(vmem_limit_bytes=40 << 20),
    )(zorder, target, safe, x, qt, keys, vt, gains, *weights, *sofar)


def second_layer(segs, zorder, targets, arrived, weights, layer=1):
    blocks = zorder.shape[0]
    _, block, width = arrived[0].shape
    per = PATCH // block
    length = blocks * block
    return pl.pallas_call(
        functools.partial(patch_kernel, segs, blocks, per),
        grid_spec=pltpu.PrefetchScalarGridSpec(
            num_scalar_prefetch=1 + segs,
            grid=(length // PATCH,),
            in_specs=[ANY] * segs + [of_layer(layer, w) for w in weights],
            out_specs=pl.BlockSpec((PATCH, width), lambda p, *_: (p, 0)),
            scratch_shapes=[
                pltpu.VMEM((PATCH, width), F32),
                pltpu.VMEM((width, width), BF16),
                pltpu.VMEM((width, width), BF16),
                pltpu.VMEM((width, PATCH), BF16),
                pltpu.VMEM((PATCH, width), BF16),
                pltpu.VMEM((width, PATCH), BF16),
                pltpu.VMEM((width, PATCH), BF16),
                pltpu.VMEM((blocks, block, width), BF16),
                SEMS((blocks,)),
            ],
        ),
        out_shape=jax.ShapeDtypeStruct((length, width), BF16),
        compiler_params=pltpu.CompilerParams(vmem_limit_bytes=40 << 20),
    )(zorder, *targets, *arrived, *weights)


def send(value, k, axis):
    n = lax.axis_size(axis)
    return lax.ppermute(value, axis, [(i, partner(i, k, n)) for i in range(n)]) if k else value


CHUNKS = (2, 4, 4)


def local(points, zorder, image, image_row, image_weight, norm_gain, in_weight, out_weight, up_weight, down_weight, hilbert_target):
    scenes = lax.axis_size("scene")
    segs = lax.axis_size("seg")
    blocks = zorder.shape[0]
    proj = dot(image, image_weight).astype(BF16)
    tables = [send(proj, k, "scene") for k in range(scenes)]
    state = joined(scenes, segs, zorder, points, image_row, tables, norm_gain, in_weight)
    weights = (out_weight, up_weight, down_weight)
    targets = [send(hilbert_target, k, "seg") for k in range(segs)]
    arrived = [None] * segs
    start = 0
    left = segs
    sofar = []
    for count in CHUNKS + (blocks,):
        count = min(count, blocks - start)
        if not count:
            break
        sofar = some_blocks(start, count, segs, left, zorder, hilbert_target, state, norm_gain, weights, sofar)
        start += count
        ready = start // CAP - (segs - left) if start < blocks else left
        for n in range(min(ready, left)):
            arrived[left - 1 - n] = send(sofar[n], left - 1 - n, "seg")
        sofar = sofar[ready:]
        left -= ready
    return second_layer(segs, zorder, targets, arrived, (norm_gain, in_weight) + weights)


def solution(mesh):
    placed = (
        P(("scene", "seg"), None),
        P(("scene", "seg")),
        P(("scene", "seg"), None),
        P(("scene", "seg")),
        P(),
        P(),
        P(),
        P(),
        P(),
        P(),
        P(("scene", "seg")),
    )
    return jax.shard_map(local, mesh=mesh, in_specs=placed, out_specs=P(("scene", "seg"), None), check_vma=False)
```
